32 devices in a mesh: rep: 2 (over x), row: 16 (over z, y, core).
Axes of the slice: x: 2, y: 2, z: 4, core: 2. Of those that a mesh axis runs over, the one named last changes fastest.
Arguments:
- weight: bfloat16 [8192, 384], P('row'), may hold values from -0.0625 to 0.0625
- first_moment: bfloat16 [2, 8192, 384], P('rep', 'row'), may hold values from -0.29882812 to 0.29882812
- second_moment: bfloat16 [2, 8192, 384], P('rep', 'row'), may hold values from 2.9921532e-05 to 0.0029907227
- token_ids: int32 [2, 4, 1024], P('rep'), may hold values from 0 to 1535
- shared_inputs: bfloat16 [1024, 8192], P(None, 'row'), may hold values from -6 to 6
- private_inputs: bfloat16 [2, 512, 8192], P('rep', None, 'row'), may hold values from -6 to 6
- shared_targets: bfloat16 [1024, 384], replicated, may hold values from -6 to 6
- private_targets: bfloat16 [2, 512, 384], P('rep'), may hold values from -6 to 6
Outputs:
- merged: float32 [8192, 384], P(('row', 'rep'))
The draws below stay inside these ranges and needn't reach their ends.
All inputs are finite; a program needn't handle non-finite values.
Results may differ from the reference program's by a relative error of at most 0.0005.
The reference program's roundings to bfloat16 on the way count: a program that leaves them out, or rounds other values in their place, can miss the bound.
Values sent between devices are 32-bit elements; how exact they have to be, the bound alone decides.
A program may use at most 64 MiB of HBM per device.

```python
import math
import jax
import jax.numpy as jnp
from jax import lax

R = 8192
C = 384
TOK = 1024
POOL = 1024
PRIV = 512
STEPS = 4
REPLICAS = 2


def with_ends(array, own_key, least, largest):
    spot = [jax.random.randint(jax.random.fold_in(own_key, axis), (), 0, length) for axis, length in enumerate(array.shape)]
    main_axis = array.shape.index(max(array.shape))
    neighbour = spot[:main_axis] + [(spot[main_axis] + 1) % array.shape[main_axis]] + spot[main_axis + 1:]
    return array.at[tuple(spot)].set(least).at[tuple(neighbour)].set(largest)


def level_of(stream_key, extent, shards, low, largest):
    def one(dim, blocks):
        steps = jax.random.uniform(jax.random.fold_in(jax.random.fold_in(stream_key, 6), dim), (blocks,), jnp.float32, low / len(shards), largest / len(shards))
        return jnp.repeat(jnp.exp(steps), extent[dim] // blocks).reshape((-1,) + (1,) * (len(extent) - dim - 1))

    factor_of = one(*shards[0])
    for cut in shards[1:]:
        factor_of = factor_of * one(*cut)
    return factor_of


def centred(stream_key, dims, scale, limit, shards=(), dtype=jnp.bfloat16):
    entries = jax.random.normal(stream_key, dims, jnp.float32) * scale
    if len(shards) > 0:
        entries = level_of(stream_key, dims, shards, -0.22, 0.18) * entries
    return jnp.clip(entries, min=-limit, max=limit).astype(dtype)


def setup_inputs(seed: int = 0) -> dict:
    splits = jax.random.split(jax.random.key(seed), 9)
    weight = centred(splits[0], (R, C), R ** -0.5, 0.0625, ((0, 16),))
    first_moment = centred(splits[1], (REPLICAS, R, C), 0.05, 0.29882812, ((0, 2), (1, 16)))
    second_moment = jnp.clip(jnp.exp(math.log(0.0029907227) - 4.604692 * jax.random.uniform(splits[2], (REPLICAS, R, C), jnp.float32) ** level_of(splits[2], (REPLICAS, R, C), ((0, 2), (1, 16)), -0.2, 0.2)), 2.9921531677246094e-05, 0.0029907227).astype(jnp.bfloat16)
    token_ids = with_ends(jax.random.randint(splits[3], (REPLICAS, STEPS, TOK), 0, POOL + PRIV), jax.random.fold_in(splits[3], 1), 0, (POOL + PRIV) - 1).astype(jnp.int32)
    shared_inputs = centred(splits[4], (POOL, R), 1.0, 6.0, ((1, 16),))
    private_inputs = centred(splits[5], (REPLICAS, PRIV, R), 1.0, 6.0, ((0, 2), (2, 16)))
    shared_targets = centred(splits[6], (POOL, C), 1.0, 6.0)
    private_targets = centred(splits[7], (REPLICAS, PRIV, C), 1.0, 6.0, ((0, 2),))
    return dict(weight=weight, first_moment=first_moment, second_moment=second_moment, token_ids=token_ids, shared_inputs=shared_inputs, private_inputs=private_inputs, shared_targets=shared_targets, private_targets=private_targets)


learn_rate = 0.001
beta_one = 0.9
beta_two = 0.95
adam_eps = 1e-08
weight_decay = 0.1
norm_eps = 1e-06

def combine_pair(lower_vec, upper_vec, cross_dot, lower_norm, upper_norm):
    lower_coef = 1.0 - cross_dot / (2.0 * (lower_norm + norm_eps))
    upper_coef = 1.0 - cross_dot / (2.0 * (upper_norm + norm_eps))
    return lower_coef * lower_vec + upper_coef * upper_vec

def reference(weight, first_moment, second_moment, token_ids, shared_inputs, private_inputs, shared_targets, private_targets):
    weight_start = weight.astype(jnp.float32)

    def replica_run(items):
        moment_one, moment_two, replica_ids, own_inputs, own_targets = items
        input_table = jnp.concatenate([shared_inputs, own_inputs], axis=0)
        target_table = jnp.concatenate([shared_targets, own_targets], axis=0)
        moment_one = moment_one.astype(jnp.float32)
        moment_two = moment_two.astype(jnp.float32)
        update_sum = jnp.zeros(weight_start.shape, jnp.float32)
        for step_index in range(STEPS):
            tok_rows = jnp.take(input_table, replica_ids[step_index], axis=0)
            targets = jnp.take(target_table, replica_ids[step_index], axis=0)
            weight_now = weight_start - learn_rate * update_sum
            weight_bf = weight_now.astype(jnp.bfloat16)
            output = jnp.dot(tok_rows, weight_bf, preferred_element_type=jnp.float32)
            residual = (output - targets.astype(jnp.float32)).astype(jnp.bfloat16)
            gradient = jnp.dot(tok_rows.T, residual, preferred_element_type=jnp.float32) / TOK
            moment_one = beta_one * moment_one + (1.0 - beta_one) * gradient
            moment_two = beta_two * moment_two + (1.0 - beta_two) * gradient * gradient
            direction = moment_one / (jnp.sqrt(moment_two) + adam_eps) + weight_decay * weight_now
            update_sum = update_sum + direction
        return update_sum
    deltas = lax.map(replica_run, (first_moment, second_moment, token_ids, private_inputs, private_targets))
    current = deltas
    while current.shape[0] > 1:
        paired = current.reshape(current.shape[0] // 2, 2, current.shape[1], current.shape[2])
        lower_vec = paired[:, 0]
        upper_vec = paired[:, 1]
        cross_dot = lax.optimization_barrier(jnp.sum(lower_vec * upper_vec, axis=(1, 2)))[:, None, None]
        lower_norm = lax.optimization_barrier(jnp.sum(lower_vec * lower_vec, axis=(1, 2)))[:, None, None]
        upper_norm = lax.optimization_barrier(jnp.sum(upper_vec * upper_vec, axis=(1, 2)))[:, None, None]
        current = combine_pair(lower_vec, upper_vec, cross_dot, lower_norm, upper_norm)
    return current[0]
```

```python
import functools

import jax
import jax.numpy as jnp
from jax import lax
from jax.experimental import pallas as pl
from jax.experimental.pallas import tpu as pltpu
from jax.sharding import PartitionSpec as P

learn_rate = 0.001
beta_one = 0.9
beta_two = 0.95
adam_eps = 1e-08
weight_decay = 0.1
norm_eps = 1e-06

LANES = 128
CORES = 2
YS = 2
PHASES = 7


def flip(index, mask):
    bit = 1
    while bit <= mask:
        if mask & bit:
            index = index + bit - 2 * bit * ((index // bit) % 2)
        bit *= 2
    return index


def train_kernel(
    zs,
    merge,
    weight,
    moment_one_in,
    moment_two_in,
    ids,
    shared_inputs,
    private_inputs,
    shared_targets,
    private_targets,
    out,
    tok,
    tok_t,
    goal,
    moment_one,
    moment_two,
    total,
    weight_b,
    away,
    acc,
    core_in,
    quarter,
    y_in,
    z_in,
    error,
    rep_in,
    dots,
    dots_in,
    send_core,
    recv_core,
    send_y,
    recv_y,
    send_z,
    recv_z,
    send_ez,
    recv_ez,
    send_ey,
    recv_ey,
    send_ec,
    recv_ec,
    send_rep,
    recv_rep,
    send_dot,
    recv_dot,
):
    steps, tokens, depth = tok.shape
    chunks = total.shape[0]
    half = tokens // CORES
    fourth = half // YS
    block = fourth // zs
    out_rows = out.shape[0]
    pool = shared_inputs.shape[0]
    priv = private_inputs.shape[0]

    rep = lax.axis_index("rep")
    row = lax.axis_index("row")
    core = row % CORES
    y = (row // CORES) % YS
    z = row // (CORES * YS)
    other_rep = 1 - rep

    core_dev = (rep, row + 1 - 2 * core)
    y_dev = (rep, row + CORES - 2 * CORES * y)
    z_peer = [flip(z, mask) for mask in range(1, zs)]
    z_dev = [(rep, row + (peer - z) * (CORES * YS)) for peer in z_peer]
    rep_dev = (other_rep, row)

    def remote(src, dst, send_sem, recv_sem, device):
        return pltpu.make_async_remote_copy(
            src_ref=src,
            dst_ref=dst,
            send_sem=send_sem,
            recv_sem=recv_sem,
            device_id=device,
            device_id_type=pl.DeviceIdType.MESH,
        )

    barrier = pltpu.get_barrier_semaphore()
    peers = [core_dev, y_dev] + z_dev + ([rep_dev] if merge else [])
    for device in peers:
        pl.semaphore_signal(
            barrier, inc=1, device_id=device, device_id_type=pl.DeviceIdType.MESH
        )

    def cols(c):
        return slice(c * LANES, (c + 1) * LANES)

    def one_hot(start, size, s, first, count):
        chosen = ids[s, pl.ds(start, size), :]
        spots = lax.broadcasted_iota(jnp.int32, (size, count), 1) + first
        return jnp.where(chosen == spots, 1.0, 0.0).astype(jnp.bfloat16)

    def pick(start, size, s, shared, private):
        return jnp.dot(
            one_hot(start, size, s, 0, pool), shared[...], preferred_element_type=jnp.float32
        ) + jnp.dot(
            one_hot(start, size, s, pool, priv), private[...], preferred_element_type=jnp.float32
        )

    piece = 256 if tokens % 256 == 0 else tokens
    pieces = tokens // piece

    def gather_piece(p, s):
        found = pick(p * piece, piece, s, shared_inputs, private_inputs)
        tok[s, pl.ds(p * piece, piece), :] = found.astype(jnp.bfloat16)
        tok_t[s, :, pl.ds(p * piece, piece)] = found.T.astype(jnp.bfloat16)

    my_row = core * half + y * fourth + z * block

    def gather_goal(s):
        goal[s] = pick(my_row, block, s, shared_targets, private_targets)

    for p in range(pieces):
        gather_piece(p, 0)
    gather_goal(0)
    tile = 128 if depth % 128 == 0 else depth
    for c in range(chunks):
        weight_b[c] = weight[:, cols(c)]
        moment_one[c] = moment_one_in[:, cols(c)].astype(jnp.float32)
        moment_two[c] = moment_two_in[:, cols(c)].astype(jnp.float32)
        total[c] = jnp.zeros((depth, LANES), jnp.float32)
    pl.semaphore_wait(barrier, len(peers))

    def copy_core(c):
        return remote(away.at[c], core_in.at[c], send_core.at[c], recv_core.at[c], core_dev)

    def copy_y(c):
        return remote(
            acc.at[c, pl.ds((1 - y) * fourth, fourth)], y_in.at[c], send_y.at[c], recv_y.at[c], y_dev
        )

    def copy_z(c, d):
        return remote(
            quarter.at[c, pl.ds(z_peer[d] * block, block)],
            z_in.at[c, d],
            send_z.at[c, d],
            recv_z.at[c, d],
            z_dev[d],
        )

    def rows_of(start, size, c):
        return error.at[c, pl.ds(start, size)]

    def spread(c, start, size, send_sem, recv_sem, device):
        return remote(rows_of(start, size, c), rows_of(start, size, c), send_sem, recv_sem, device)

    def send_err_z(c, d):
        return spread(c, my_row, block, send_ez.at[c, d], recv_ez.at[c, d], z_dev[d])

    def land_err_z(c, d):
        start = core * half + y * fourth + z_peer[d] * block
        return spread(c, start, block, send_ez.at[c, d], recv_ez.at[c, d], z_dev[d])

    def send_err_y(c):
        return spread(c, core * half + y * fourth, fourth, send_ey.at[c], recv_ey.at[c], y_dev)

    def land_err_y(c):
        return spread(c, core * half + (1 - y) * fourth, fourth, send_ey.at[c], recv_ey.at[c], y_dev)

    def send_err_core(c):
        return spread(c, core * half, half, send_ec.at[c], recv_ec.at[c], core_dev)

    def land_err_core(c):
        return spread(c, (1 - core) * half, half, send_ec.at[c], recv_ec.at[c], core_dev)

    def copy_rep(c):
        return remote(
            total.at[c, pl.ds(other_rep * out_rows, out_rows)],
            rep_in.at[c],
            send_rep.at[c],
            recv_rep.at[c],
            rep_dev,
        )

    def phase_0(c, s):
        away[c] = jnp.dot(
            tok[s, pl.ds((1 - core) * half, half), :], weight_b[c], preferred_element_type=jnp.float32
        )
        copy_core(c).start()
        acc[c] = jnp.dot(
            tok[s, pl.ds(core * half, half), :], weight_b[c], preferred_element_type=jnp.float32
        )

    def phase_1(c, s):
        copy_core(c).wait()
        theirs = pl.ds((1 - y) * fourth, fourth)
        acc[c, theirs, :] = acc[c, theirs, :] + core_in[c, theirs, :]
        copy_y(c).start()
        mine = pl.ds(y * fourth, fourth)
        quarter[c] = acc[c, mine, :] + core_in[c, mine, :]

    def phase_2(c, s):
        copy_y(c).wait()
        quarter[c] = quarter[c] + y_in[c]
        for d in range(zs - 1):
            copy_z(c, d).start()

    def phase_3(c, s):
        value = quarter[c, pl.ds(z * block, block), :]
        for d in range(zs - 1):
            copy_z(c, d).wait()
            value = value + z_in[c, d]
        residual = (value - goal[s, :, cols(c)]).astype(jnp.bfloat16)
        error[c, pl.ds(my_row, block), :] = residual.astype(jnp.float32)
        for d in range(zs - 1):
            send_err_z(c, d).start()

    def phase_4(c, s):
        for d in range(zs - 1):
            land_err_z(c, d).wait_recv()
        send_err_y(c).start()

    def phase_5(c, s):
        land_err_y(c).wait_recv()
        send_err_core(c).start()

    def phase_6(c, s):
        land_err_core(c).wait_recv()
        residual = error[c].astype(jnp.bfloat16)
        for t in range(depth // tile):
            at = slice(t * tile, (t + 1) * tile)
            gradient = jnp.dot(
                tok_t[s, at, :], residual, preferred_element_type=jnp.float32
            ) / tokens
            start = weight[at, cols(c)].astype(jnp.float32)
            so_far = total[c, at, :]
            m = beta_one * moment_one[c, at, :] + (1.0 - beta_one) * gradient
            v = beta_two * moment_two[c, at, :] + (1.0 - beta_two) * gradient * gradient
            moment_one[c, at, :] = m
            moment_two[c, at, :] = v
            weight_now = start - learn_rate * so_far
            so_far = so_far + (m / (jnp.sqrt(v) + adam_eps) + weight_decay * weight_now)
            total[c, at, :] = so_far
            weight_b[c, at, :] = (start - learn_rate * so_far).astype(jnp.bfloat16)
        for d in range(zs - 1):
            send_err_z(c, d).wait_send()
        send_err_y(c).wait_send()
        send_err_core(c).wait_send()

        if merge:

            @pl.when(s == steps - 1)
            def _():
                copy_rep(c).start()

    phases = (phase_0, phase_1, phase_2, phase_3, phase_4, phase_5, phase_6)
    gap = PHASES // chunks if chunks <= PHASES else 1

    def one_step(s, carry):
        for slot in range(PHASES):
            for c in range(chunks):
                late = slot - gap * c
                back = -(late // PHASES)
                phase = phases[late % PHASES]

                @pl.when(jnp.logical_and(s - back >= 0, s - back < steps))
                def _(c=c, back=back, phase=phase):
                    phase(c, s - back)

            for p in range(pieces):
                if slot == min(1 + p, PHASES - 1):

                    @pl.when(s + 1 < steps)
                    def _(p=p):
                        gather_piece(p, s + 1)

            if slot == PHASES - 2:

                @pl.when(s + 1 < steps)
                def _():
                    gather_goal(s + 1)

        return carry

    extra = -(-(gap * (chunks - 1)) // PHASES)
    lax.fori_loop(0, steps + extra, one_step, 0)

    if not merge:
        for c in range(chunks):
            out[:, cols(c)] = total[c]
        return

    zero = jnp.zeros((8, LANES), jnp.float32)
    cross, own_norm, other_norm = zero, zero, zero

    def fold(values):
        return jnp.sum(values.reshape(out_rows // 8, 8, LANES), axis=0)

    mine = pl.ds(rep * out_rows, out_rows)
    for c in range(chunks):
        copy_rep(c).wait()
        own, far = total[c, mine, :], rep_in[c]
        cross = cross + fold(own * far)
        own_norm = own_norm + fold(own * own)
        other_norm = other_norm + fold(far * far)
    swap = jnp.full((8, LANES), rep, jnp.int32) == 1
    sums = [
        cross,
        jnp.where(swap, other_norm, own_norm),
        jnp.where(swap, own_norm, other_norm),
    ]
    stages = [[rep_dev], [core_dev], [y_dev], z_dev]
    slot = 0
    for number, devices in enumerate(stages):
        for k in range(3):
            dots[number, k] = sums[k]
        copies = []
        for device in devices:
            copies.append(
                remote(
                    dots.at[number],
                    dots_in.at[slot],
                    send_dot.at[slot],
                    recv_dot.at[slot],
                    device,
                )
            )
            slot += 1
        for copy in copies:
            copy.start()
        for place, copy in enumerate(copies):
            copy.wait()
            for k in range(3):
                sums[k] = sums[k] + dots_in[slot - len(copies) + place, k]
    cross, lower, upper = [jnp.sum(s, axis=(0, 1), keepdims=True) for s in sums]
    lower_coef = 1.0 - cross / (2.0 * (lower + norm_eps))
    upper_coef = 1.0 - cross / (2.0 * (upper + norm_eps))
    first = jnp.full((1, 1), rep, jnp.int32) == 0
    own_coef = jnp.where(first, lower_coef, upper_coef)
    far_coef = jnp.where(first, upper_coef, lower_coef)
    for c in range(chunks):
        out[:, cols(c)] = own_coef * total[c, mine, :] + far_coef * rep_in[c]


def from_partner(block, axis, bit):
    count = lax.axis_size(axis)
    route = []
    for low in range(count):
        high = low | 1 << bit
        if high != low and high < count:
            route += [(low, high), (high, low)]
    return lax.ppermute(block, axis, route)


def merge_tree(current):
    replica_count = lax.axis_size("rep")
    level_count = replica_count.bit_length() - 1
    replica = lax.axis_index("rep")
    block_rows = current.shape[0] // replica_count
    for tree_level in range(level_count):
        own_bit = replica // 2**tree_level % 2
        received = from_partner(current, "rep", tree_level)
        lower_vec = jnp.where(own_bit == 0, current, received)
        upper_vec = jnp.where(own_bit == 0, received, current)
        cross_dot, lower_norm, upper_norm = lax.psum(
            (
                jnp.sum(lower_vec * upper_vec),
                jnp.sum(lower_vec * lower_vec),
                jnp.sum(upper_vec * upper_vec),
            ),
            "row",
        )
        lower_coef = 1.0 - cross_dot / (2.0 * (lower_norm + norm_eps))
        upper_coef = 1.0 - cross_dot / (2.0 * (upper_norm + norm_eps))
        current = lower_coef * lower_vec + upper_coef * upper_vec
    return lax.dynamic_slice_in_dim(current, replica * block_rows, block_rows, 0)


def solution(mesh):
    rows = mesh.shape["row"]
    zs = rows // (CORES * YS)
    merge = mesh.shape["rep"] == 2

    def on_device(
        weight,
        first_moment,
        second_moment,
        token_ids,
        shared_inputs,
        private_inputs,
        shared_targets,
        private_targets,
    ):
        depth, columns = weight.shape
        steps, tokens = token_ids.shape[1:]
        chunks = columns // LANES
        half = tokens // CORES
        fourth = half // YS
        block = fourth // zs
        out_rows = depth // 2 if merge else depth
        links = zs - 1 + 3
        dma = pltpu.SemaphoreType.DMA
        f32 = jnp.float32
        pair = [dma((chunks,)), dma((chunks,))]
        pair_z = [dma((chunks, zs - 1)), dma((chunks, zs - 1))]
        result = pl.pallas_call(
            functools.partial(train_kernel, zs, merge),
            out_shape=jax.ShapeDtypeStruct((out_rows, columns), f32),
            in_specs=[pl.BlockSpec(memory_space=pltpu.VMEM)] * 8,
            out_specs=pl.BlockSpec(memory_space=pltpu.VMEM),
            scratch_shapes=[
                pltpu.VMEM((steps, tokens, depth), jnp.bfloat16),
                pltpu.VMEM((steps, depth, tokens), jnp.bfloat16),
                pltpu.VMEM((steps, block, columns), f32),
                pltpu.VMEM((chunks, depth, LANES), f32),
                pltpu.VMEM((chunks, depth, LANES), f32),
                pltpu.VMEM((chunks, depth, LANES), f32),
                pltpu.VMEM((chunks, depth, LANES), jnp.bfloat16),
                pltpu.VMEM((chunks, half, LANES), f32),
                pltpu.VMEM((chunks, half, LANES), f32),
                pltpu.VMEM((chunks, half, LANES), f32),
                pltpu.VMEM((chunks, fourth, LANES), f32),
                pltpu.VMEM((chunks, fourth, LANES), f32),
                pltpu.VMEM((chunks, zs - 1, block, LANES), f32),
                pltpu.VMEM((chunks, tokens, LANES), f32),
                pltpu.VMEM((chunks, out_rows, LANES), f32),
                pltpu.VMEM((4, 3, 8, LANES), f32),
                pltpu.VMEM((links, 3, 8, LANES), f32),
            ]
            + pair
            + pair
            + pair_z
            + pair_z
            + pair
            + pair
            + pair
            + [dma((links,)), dma((links,))],
            compiler_params=pltpu.CompilerParams(
                collective_id=0, has_side_effects=True, vmem_limit_bytes=56 * 1024 * 1024
            ),
        )(
            weight,
            first_moment[0],
            second_moment[0],
            token_ids[0][:, :, None],
            shared_inputs,
            private_inputs[0],
            shared_targets,
            private_targets[0],
        )
        return result if merge else merge_tree(result)

    placed = (
        P("row", None),
        P("rep", "row", None),
        P("rep", "row", None),
        P("rep", None, None),
        P(None, "row"),
        P("rep", None, "row"),
        P(),
        P("rep", None, None),
    )
    return jax.shard_map(
        on_device, mesh=mesh, in_specs=placed, out_specs=P(("row", "rep"), None), check_vma=False
    )
```

```python
import functools

import jax
import jax.numpy as jnp
from jax import lax
from jax.experimental import pallas as pl
from jax.experimental.pallas import tpu as pltpu
from jax.sharding import PartitionSpec as P

learn_rate = 0.001
beta_one = 0.9
beta_two = 0.95
adam_eps = 1e-08
weight_decay = 0.1
norm_eps = 1e-06

LANES = 128
CORES = 2
YS = 2
PHASES = 7


def flip(index, mask):
    bit = 1
    while bit <= mask:
        if mask & bit:
            index = index + bit - 2 * bit * ((index // bit) % 2)
        bit *= 2
    return index


def train_kernel(
    zs,
    merge,
    weight,
    moment_one_in,
    moment_two_in,
    ids,
    shared_inputs,
    private_inputs,
    shared_targets,
    private_targets,
    out,
    tok,
    tok_t,
    goal,
    moment_one,
    moment_two,
    total,
    weight_b,
    away,
    acc,
    core_in,
    quarter,
    y_in,
    z_in,
    error,
    rep_in,
    dots,
    dots_in,
    send_core,
    recv_core,
    send_y,
    recv_y,
    send_z,
    recv_z,
    send_ez,
    recv_ez,
    send_ey,
    recv_ey,
    send_ec,
    recv_ec,
    send_rep,
    recv_rep,
    send_dot,
    recv_dot,
):
    steps, tokens, depth = tok.shape
    chunks = total.shape[0]
    half = tokens // CORES
    fourth = half // YS
    block = fourth // zs
    out_rows = out.shape[0]
    pool = shared_inputs.shape[0]
    priv = private_inputs.shape[0]

    rep = lax.axis_index("rep")
    row = lax.axis_index("row")
    core = row % CORES
    y = (row // CORES) % YS
    z = row // (CORES * YS)
    other_rep = 1 - rep

    core_dev = (rep, row + 1 - 2 * core)
    y_dev = (rep, row + CORES - 2 * CORES * y)
    z_peer = [flip(z, mask) for mask in range(1, zs)]
    z_dev = [(rep, row + (peer - z) * (CORES * YS)) for peer in z_peer]
    rep_dev = (other_rep, row)

    def remote(src, dst, send_sem, recv_sem, device):
        return pltpu.make_async_remote_copy(
            src_ref=src,
            dst_ref=dst,
            send_sem=send_sem,
            recv_sem=recv_sem,
            device_id=device,
            device_id_type=pl.DeviceIdType.MESH,
        )

    barrier = pltpu.get_barrier_semaphore()
    peers = [core_dev, y_dev] + z_dev + ([rep_dev] if merge else [])
    for device in peers:
        pl.semaphore_signal(
            barrier, inc=1, device_id=device, device_id_type=pl.DeviceIdType.MESH
        )

    def cols(c):
        return slice(c * LANES, (c + 1) * LANES)

    def one_hot(start, size, s, first, count):
        chosen = ids[s, pl.ds(start, size), :]
        spots = lax.broadcasted_iota(jnp.int32, (size, count), 1) + first
        return jnp.where(chosen == spots, 1.0, 0.0).astype(jnp.bfloat16)

    def pick(start, size, s, shared, private):
        return jnp.dot(
            one_hot(start, size, s, 0, pool), shared[...], preferred_element_type=jnp.float32
        ) + jnp.dot(
            one_hot(start, size, s, pool, priv), private[...], preferred_element_type=jnp.float32
        )

    piece = 256 if tokens % 256 == 0 else tokens
    pieces = tokens // piece

    def gather_piece(p, s):
        found = pick(p * piece, piece, s, shared_inputs, private_inputs)
        tok[s, pl.ds(p * piece, piece), :] = found.astype(jnp.bfloat16)
        tok_t[s, :, pl.ds(p * piece, piece)] = found.T.astype(jnp.bfloat16)

    my_row = core * half + y * fourth + z * block

    def gather_goal(s):
        goal[s] = pick(my_row, block, s, shared_targets, private_targets)

    for p in range(pieces):
        gather_piece(p, 0)
    gather_goal(0)
    tile = 128 if depth % 128 == 0 else depth
    for c in range(chunks):
        weight_b[c] = weight[:, cols(c)]
        moment_one[c] = moment_one_in[:, cols(c)].astype(jnp.float32)
        moment_two[c] = moment_two_in[:, cols(c)].astype(jnp.float32)
        total[c] = jnp.zeros((depth, LANES), jnp.float32)
    pl.semaphore_wait(barrier, len(peers))

    z_order = z_peer + [z]

    def copy_core(c, k):
        if k < zs:
            at = pl.ds((1 - y) * fourth + z_order[k] * block, block)
        else:
            at = pl.ds(y * fourth, fourth)
        return remote(
            away.at[c, at], core_in.at[c, at], send_core.at[c, k], recv_core.at[c, k], core_dev
        )

    def copy_y(c, k):
        at = pl.ds((1 - y) * fourth + z_order[k] * block, block)
        return remote(
            acc.at[c, at],
            y_in.at[c, pl.ds(z_order[k] * block, block)],
            send_y.at[c, k],
            recv_y.at[c, k],
            y_dev,
        )

    def copy_z(c, d):
        return remote(
            quarter.at[c, pl.ds(z_peer[d] * block, block)],
            z_in.at[c, d],
            send_z.at[c, d],
            recv_z.at[c, d],
            z_dev[d],
        )

    def spread(c, start, send_sem, recv_sem, device):
        at = error.at[c, pl.ds(start, block)]
        return remote(at, at, send_sem, recv_sem, device)

    def place_of(core_at, y_at, z_at):
        return core_at * half + y_at * fourth + z_at * block

    def send_err_z(c, d):
        return spread(c, my_row, send_ez.at[c, d], recv_ez.at[c, d], z_dev[d])

    def land_err_z(c, d):
        start = place_of(core, y, z_peer[d])
        return spread(c, start, send_ez.at[c, d], recv_ez.at[c, d], z_dev[d])

    def send_err_y(c, k):
        start = place_of(core, y, z_order[k])
        return spread(c, start, send_ey.at[c, k], recv_ey.at[c, k], y_dev)

    def land_err_y(c, k):
        start = place_of(core, 1 - y, z_order[k])
        return spread(c, start, send_ey.at[c, k], recv_ey.at[c, k], y_dev)

    def send_err_core(c, side, k):
        n = side * zs + k
        start = place_of(core, y + side * (1 - 2 * y), z_order[k])
        return spread(c, start, send_ec.at[c, n], recv_ec.at[c, n], core_dev)

    def land_err_core(c, side, k):
        n = side * zs + k
        start = place_of(1 - core, y + side * (1 - 2 * y), z_order[k])
        return spread(c, start, send_ec.at[c, n], recv_ec.at[c, n], core_dev)

    def copy_rep(c):
        return remote(
            total.at[c, pl.ds(other_rep * out_rows, out_rows)],
            rep_in.at[c],
            send_rep.at[c],
            recv_rep.at[c],
            rep_dev,
        )

    def forward(c, s, core_at, y_at):
        start = core_at * half + y_at * fourth
        return jnp.dot(
            tok[s, pl.ds(start, fourth), :], weight_b[c], preferred_element_type=jnp.float32
        )

    def phase_0(c, s):
        away[c, pl.ds((1 - y) * fourth, fourth), :] = forward(c, s, 1 - core, 1 - y)
        for k in range(zs):
            copy_core(c, k).start()
        away[c, pl.ds(y * fourth, fourth), :] = forward(c, s, 1 - core, y)
        copy_core(c, zs).start()
        acc[c, pl.ds((1 - y) * fourth, fourth), :] = forward(c, s, core, 1 - y)
        acc[c, pl.ds(y * fourth, fourth), :] = forward(c, s, core, y)

    def phase_1(c, s):
        for k in range(zs):
            copy_core(c, k).wait()
            at = pl.ds((1 - y) * fourth + z_order[k] * block, block)
            acc[c, at, :] = acc[c, at, :] + core_in[c, at, :]
            copy_y(c, k).start()

    def phase_2(c, s):
        copy_core(c, zs).wait()
        for k in range(zs):
            copy_y(c, k).wait()
            at = pl.ds(z_order[k] * block, block)
            own = pl.ds(y * fourth + z_order[k] * block, block)
            quarter[c, at, :] = acc[c, own, :] + core_in[c, own, :] + y_in[c, at, :]
            if k < zs - 1:
                copy_z(c, k).start()

    def phase_3(c, s):
        value = quarter[c, pl.ds(z * block, block), :]
        for d in range(zs - 1):
            copy_z(c, d).wait()
            value = value + z_in[c, d]
        residual = (value - goal[s, :, cols(c)]).astype(jnp.bfloat16)
        error[c, pl.ds(my_row, block), :] = residual.astype(jnp.float32)
        for d in range(zs - 1):
            send_err_z(c, d).start()
        send_err_y(c, zs - 1).start()
        send_err_core(c, 0, zs - 1).start()

    def phase_4(c, s):
        for d in range(zs - 1):
            land_err_z(c, d).wait_recv()
            send_err_y(c, d).start()
            send_err_core(c, 0, d).start()

    early_first = [zs - 1] + list(range(zs - 1))

    def phase_5(c, s):
        for k in early_first:
            land_err_y(c, k).wait_recv()
            send_err_core(c, 1, k).start()

    def phase_6(c, s):
        for side in range(YS):
            for k in early_first:
                land_err_core(c, side, k).wait_recv()
        residual = error[c].astype(jnp.bfloat16)
        for t in range(depth // tile):
            at = slice(t * tile, (t + 1) * tile)
            gradient = jnp.dot(
                tok_t[s, at, :], residual, preferred_element_type=jnp.float32
            ) / tokens
            start = weight[at, cols(c)].astype(jnp.float32)
            so_far = total[c, at, :]
            m = beta_one * moment_one[c, at, :] + (1.0 - beta_one) * gradient
            v = beta_two * moment_two[c, at, :] + (1.0 - beta_two) * gradient * gradient
            moment_one[c, at, :] = m
            moment_two[c, at, :] = v
            weight_now = start - learn_rate * so_far
            so_far = so_far + (m / (jnp.sqrt(v) + adam_eps) + weight_decay * weight_now)
            total[c, at, :] = so_far
            weight_b[c, at, :] = (start - learn_rate * so_far).astype(jnp.bfloat16)
        for d in range(zs - 1):
            send_err_z(c, d).wait_send()
        for k in range(zs):
            send_err_y(c, k).wait_send()
            for side in range(YS):
                send_err_core(c, side, k).wait_send()

        if merge:

            @pl.when(s == steps - 1)
            def _():
                copy_rep(c).start()

    phases = (phase_0, phase_1, phase_2, phase_3, phase_4, phase_5, phase_6)
    gap = PHASES // chunks if chunks <= PHASES else 1

    def one_step(s, carry):
        for slot in range(PHASES):
            for c in range(chunks):
                late = slot - gap * c
                back = -(late // PHASES)
                phase = phases[late % PHASES]

                @pl.when(jnp.logical_and(s - back >= 0, s - back < steps))
                def _(c=c, back=back, phase=phase):
                    phase(c, s - back)

            for p in range(pieces):
                if slot == min(1 + p, PHASES - 1):

                    @pl.when(s + 1 < steps)
                    def _(p=p):
                        gather_piece(p, s + 1)

            if slot == PHASES - 2:

                @pl.when(s + 1 < steps)
                def _():
                    gather_goal(s + 1)

        return carry

    extra = -(-(gap * (chunks - 1)) // PHASES)
    lax.fori_loop(0, steps + extra, one_step, 0)

    if not merge:
        for c in range(chunks):
            out[:, cols(c)] = total[c]
        return

    zero = jnp.zeros((8, LANES), jnp.float32)
    cross, own_norm, other_norm = zero, zero, zero

    def fold(values):
        return jnp.sum(values.reshape(out_rows // 8, 8, LANES), axis=0)

    mine = pl.ds(rep * out_rows, out_rows)
    for c in range(chunks):
        copy_rep(c).wait()
        own, far = total[c, mine, :], rep_in[c]
        cross = cross + fold(own * far)
        own_norm = own_norm + fold(own * own)
        other_norm = other_norm + fold(far * far)
    swap = jnp.full((8, LANES), rep, jnp.int32) == 1
    sums = [
        cross,
        jnp.where(swap, other_norm, own_norm),
        jnp.where(swap, own_norm, other_norm),
    ]
    stages = [[rep_dev], [core_dev], [y_dev], z_dev]
    slot = 0
    for number, devices in enumerate(stages):
        for k in range(3):
            dots[number, k] = sums[k]
        copies = []
        for device in devices:
            copies.append(
                remote(
                    dots.at[number],
                    dots_in.at[slot],
                    send_dot.at[slot],
                    recv_dot.at[slot],
                    device,
                )
            )
            slot += 1
        for copy in copies:
            copy.start()
        for place, copy in enumerate(copies):
            copy.wait()
            for k in range(3):
                sums[k] = sums[k] + dots_in[slot - len(copies) + place, k]
    cross, lower, upper = [jnp.sum(s, axis=(0, 1), keepdims=True) for s in sums]
    lower_coef = 1.0 - cross / (2.0 * (lower + norm_eps))
    upper_coef = 1.0 - cross / (2.0 * (upper + norm_eps))
    first = jnp.full((1, 1), rep, jnp.int32) == 0
    own_coef = jnp.where(first, lower_coef, upper_coef)
    far_coef = jnp.where(first, upper_coef, lower_coef)
    for c in range(chunks):
        out[:, cols(c)] = own_coef * total[c, mine, :] + far_coef * rep_in[c]


def from_partner(block, axis, bit):
    count = lax.axis_size(axis)
    route = []
    for low in range(count):
        high = low | 1 << bit
        if high != low and high < count:
            route += [(low, high), (high, low)]
    return lax.ppermute(block, axis, route)


def merge_tree(current):
    replica_count = lax.axis_size("rep")
    level_count = replica_count.bit_length() - 1
    replica = lax.axis_index("rep")
    block_rows = current.shape[0] // replica_count
    for tree_level in range(level_count):
        own_bit = replica // 2**tree_level % 2
        received = from_partner(current, "rep", tree_level)
        lower_vec = jnp.where(own_bit == 0, current, received)
        upper_vec = jnp.where(own_bit == 0, received, current)
        cross_dot, lower_norm, upper_norm = lax.psum(
            (
                jnp.sum(lower_vec * upper_vec),
                jnp.sum(lower_vec * lower_vec),
                jnp.sum(upper_vec * upper_vec),
            ),
            "row",
        )
        lower_coef = 1.0 - cross_dot / (2.0 * (lower_norm + norm_eps))
        upper_coef = 1.0 - cross_dot / (2.0 * (upper_norm + norm_eps))
        current = lower_coef * lower_vec + upper_coef * upper_vec
    return lax.dynamic_slice_in_dim(current, replica * block_rows, block_rows, 0)


def solution(mesh):
    rows = mesh.shape["row"]
    zs = rows // (CORES * YS)
    merge = mesh.shape["rep"] == 2

    def on_device(
        weight,
        first_moment,
        second_moment,
        token_ids,
        shared_inputs,
        private_inputs,
        shared_targets,
        private_targets,
    ):
        depth, columns = weight.shape
        steps, tokens = token_ids.shape[1:]
        chunks = columns // LANES
        half = tokens // CORES
        fourth = half // YS
        block = fourth // zs
        out_rows = depth // 2 if merge else depth
        links = zs - 1 + 3
        dma = pltpu.SemaphoreType.DMA
        f32 = jnp.float32

        def pair_of(count):
            return [dma((chunks, count)), dma((chunks, count))]

        result = pl.pallas_call(
            functools.partial(train_kernel, zs, merge),
            out_shape=jax.ShapeDtypeStruct((out_rows, columns), f32),
            in_specs=[pl.BlockSpec(memory_space=pltpu.VMEM)] * 8,
            out_specs=pl.BlockSpec(memory_space=pltpu.VMEM),
            scratch_shapes=[
                pltpu.VMEM((steps, tokens, depth), jnp.bfloat16),
                pltpu.VMEM((steps, depth, tokens), jnp.bfloat16),
                pltpu.VMEM((steps, block, columns), f32),
                pltpu.VMEM((chunks, depth, LANES), f32),
                pltpu.VMEM((chunks, depth, LANES), f32),
                pltpu.VMEM((chunks, depth, LANES), f32),
                pltpu.VMEM((chunks, depth, LANES), jnp.bfloat16),
                pltpu.VMEM((chunks, half, LANES), f32),
                pltpu.VMEM((chunks, half, LANES), f32),
                pltpu.VMEM((chunks, half, LANES), f32),
                pltpu.VMEM((chunks, fourth, LANES), f32),
                pltpu.VMEM((chunks, fourth, LANES), f32),
                pltpu.VMEM((chunks, zs - 1, block, LANES), f32),
                pltpu.VMEM((chunks, tokens, LANES), f32),
                pltpu.VMEM((chunks, out_rows, LANES), f32),
                pltpu.VMEM((4, 3, 8, LANES), f32),
                pltpu.VMEM((links, 3, 8, LANES), f32),
            ]
            + pair_of(zs + 1)
            + pair_of(zs)
            + pair_of(zs - 1)
            + pair_of(zs - 1)
            + pair_of(zs)
            + pair_of(YS * zs)
            + [dma((chunks,)), dma((chunks,))]
            + [dma((links,)), dma((links,))],
            compiler_params=pltpu.CompilerParams(
                collective_id=0, has_side_effects=True, vmem_limit_bytes=56 * 1024 * 1024
            ),
        )(
            weight,
            first_moment[0],
            second_moment[0],
            token_ids[0][:, :, None],
            shared_inputs,
            private_inputs[0],
            shared_targets,
            private_targets[0],
        )
        return result if merge else merge_tree(result)

    placed = (
        P("row", None),
        P("rep", "row", None),
        P("rep", "row", None),
        P("rep", None, None),
        P(None, "row"),
        P("rep", None, "row"),
        P(),
        P("rep", None, None),
    )
    return jax.shard_map(
        on_device, mesh=mesh, in_specs=placed, out_specs=P(("row", "rep"), None), check_vma=False
    )
```
